32 devices in a mesh: gx: 16 (over z, y, x), gy: 2 (over core).
Axes of the slice: x: 2, y: 2, z: 4, core: 2. Of those that a mesh axis runs over, the one named last changes fastest.
Arguments:
- forward_coeff: float32 [192, 4096], P(None, ('gx', 'gy')), may hold values from -6 to 6
- incident: float32 [192, 4096], P(None, ('gx', 'gy')), may hold values from -6 to 6
- cost_grad: float32 [192, 4096], P(None, ('gx', 'gy')), may hold values from -6 to 6
- tmat_real: float32 [4, 96, 96], replicated, may hold values from -0.21875 to 0.21875
- tmat_imag: float32 [4, 96, 96], replicated, may hold values from -0.21875 to 0.21875
- translation_real: float32 [10, 96, 96], replicated, may hold values from -0.125 to 0.125
- translation_imaginary: float32 [10, 96, 96], replicated, may hold values from -0.125 to 0.125
- neighbours: int32 [10, 4096], P(None, ('gx', 'gy')), may hold values from -1 to 4095, as said below
- particle_type: int32 [4096], P(('gx', 'gy')), may hold values from 0 to 3
Outputs:
- adjoint: float32 [192, 4096], P(None, ('gx', 'gy'))
- sensitivity: float32 [4, 192, 192], replicated
The draws below stay inside these ranges and needn't reach their ends.
Inputs may be any that keep to these rules, and one draw needn't show every extreme that they name: `neighbours`: particles sit on a lattice cut into spatial tiles of 4 rows (wide direction) by 32 columns (short direction); tile t holds slots t * 128 to t * 128 + 127, tiles numbered along the short direction fastest, and slot p of a tile sits at row p // 32 and column p % 32 of its tile. An entry of -1 marks an empty slot. Any other entry names a particle whose lattice row and column differ from the particle's own by dr and dc with 0 < dr^2 + dc^2 <= 5; the entries of one particle's list name distinct particles.
All inputs are finite; a program needn't handle non-finite values.
Results may differ from the reference program's by a relative error of at most 0.0001.
Values sent between devices are 32-bit elements; how exact they have to be, the bound alone decides.
A program may use at most 64 MiB of HBM per device.

```python
import jax
import jax.numpy as jnp
from jax import lax

COEFFICIENT_SIZE = 96
COEFFICIENT_REAL = 192
NEIGHBOUR_SLOTS = 10
TYPES = 4
KRYLOV = 2
TROWS = 4
TCOLS = 32
PDEV = 128
NPART = 4096
N_GX = 16
N_GY = 2


def draw_neighbours(key, part):
    total_count = PDEV * N_GX * N_GY
    particle_ids = jnp.arange(total_count, dtype=jnp.int32)
    tile_index = particle_ids // PDEV
    tile_row = tile_index // N_GY
    tile_col = tile_index % N_GY
    own_slot = particle_ids % PDEV
    site_row = tile_row * TROWS + own_slot // TCOLS
    site_col = tile_col * TCOLS + own_slot % TCOLS
    reach_row = jnp.array([1, -1, 0, 0, 1, 1, -1, -1, 2, -2, 0, 0, 2, 2, -2, -2, 1, 1, -1, -1], dtype=jnp.int32)
    reach_col = jnp.array([0, 0, 1, -1, 1, -1, 1, -1, 0, 0, 2, -2, 1, -1, 1, -1, 2, -2, 2, -2], dtype=jnp.int32)
    random_subkeys = jax.random.split(jax.random.fold_in(key, 17), 2)
    ranking_values = jax.random.randint(random_subkeys[0], (20, total_count), 0, 2 ** 20) * 32 + jnp.arange(20, dtype=jnp.int32)[:, None]
    selected_entries = jnp.argsort(ranking_values, axis=0)[:NEIGHBOUR_SLOTS].astype(jnp.int32)
    new_row = site_row[None, :] + jnp.take(reach_row, selected_entries)
    new_col = site_col[None, :] + jnp.take(reach_col, selected_entries)
    inside = (new_row >= 0) & (new_row < N_GX * TROWS) & (new_col >= 0) & (new_col < N_GY * TCOLS)
    safe_row = jnp.where(inside, new_row, 0)
    safe_col = jnp.where(inside, new_col, 0)
    final_output = (safe_row // TROWS * N_GY + safe_col // TCOLS) * PDEV + safe_row % TROWS * TCOLS + safe_col % TCOLS
    empty_slots = jax.random.randint(random_subkeys[1], (NEIGHBOUR_SLOTS, total_count), 0, 5) == 0
    final_output = jnp.where(inside & jnp.logical_not(empty_slots), final_output, -1).astype(jnp.int32)
    last_list = final_output[:, total_count - 2]
    last_list = jnp.where(last_list == total_count - 1, -1, last_list).at[0].set(total_count - 1)
    final_output = final_output.at[:, total_count - 2].set(last_list)
    final_output = final_output.at[NEIGHBOUR_SLOTS - 1, 0].set(-1)
    return final_output.astype(jnp.int32)


def with_ends(result, own_key, low, top_value):
    shape = result.shape
    place = [jax.random.randint(jax.random.fold_in(own_key, axis), (), 0, shape[axis]) for axis in range(len(shape))]
    result = result.at[tuple(place)].set(low)
    longest = shape.index(max(shape))
    place[longest] = (place[longest] + 1) % shape[longest]
    return result.at[tuple(place)].set(top_value)


def shard_levels(own_key, extent, cuts, smallest, largest):
    gain = 1.0
    for axis_at, shards_of in cuts:
        heights = jax.random.uniform(jax.random.fold_in(jax.random.fold_in(own_key, 6), axis_at), (shards_of,), jnp.float32, smallest / len(cuts), largest / len(cuts))
        gain = gain * jnp.repeat(jnp.exp(heights), extent[axis_at] // shards_of).reshape((-1,) + (1,) * (len(extent) - 1 - axis_at))
    return gain


def noise(rng, dims, scale, bound, pieces=(), held_as=jnp.bfloat16):
    values = scale * jax.random.normal(rng, dims, jnp.float32)
    if pieces:
        values = values * shard_levels(rng, dims, pieces, -0.22, 0.18)
    return jnp.clip(values, -bound, bound).astype(held_as)


def setup_inputs(seed: int = 0) -> dict:
    arg_keys = jax.random.split(jax.random.key(seed), 10)
    forward_coeff = noise(arg_keys[0], (COEFFICIENT_REAL, NPART), 1.0, 6.0, ((1, 32),), jnp.float32)
    incident = noise(arg_keys[1], (COEFFICIENT_REAL, NPART), 1.0, 6.0, ((1, 32),), jnp.float32)
    cost_grad = noise(arg_keys[2], (COEFFICIENT_REAL, NPART), 1.0, 6.0, ((1, 32),), jnp.float32)
    tmat_real = noise(arg_keys[3], (TYPES, COEFFICIENT_SIZE, COEFFICIENT_SIZE), (4 * COEFFICIENT_REAL) ** -0.5, 0.21875, (), jnp.float32)
    tmat_imag = noise(arg_keys[4], (TYPES, COEFFICIENT_SIZE, COEFFICIENT_SIZE), (4 * COEFFICIENT_REAL) ** -0.5, 0.21875, (), jnp.float32)
    translation_real = noise(arg_keys[5], (NEIGHBOUR_SLOTS, COEFFICIENT_SIZE, COEFFICIENT_SIZE), (12 * COEFFICIENT_REAL) ** -0.5, 0.125, (), jnp.float32)
    translation_imaginary = noise(arg_keys[6], (NEIGHBOUR_SLOTS, COEFFICIENT_SIZE, COEFFICIENT_SIZE), (12 * COEFFICIENT_REAL) ** -0.5, 0.125, (), jnp.float32)
    neighbours = draw_neighbours(jax.random.fold_in(arg_keys[9], 71), 0)
    particle_type = with_ends(jax.random.randint(arg_keys[8], (NPART,), 0, TYPES), jax.random.fold_in(arg_keys[8], 1), 0, TYPES - 1).astype(jnp.int32)
    return {"forward_coeff": forward_coeff, "incident": incident, "cost_grad": cost_grad, "tmat_real": tmat_real, "tmat_imag": tmat_imag, "translation_real": translation_real, "translation_imaginary": translation_imaginary, "neighbours": neighbours, "particle_type": particle_type}


HIGH = lax.Precision.HIGHEST

def complex_blocks(real_part, imag_part):
    upper_rows = jnp.concatenate([real_part, -imag_part], axis=2)
    lower_rows = jnp.concatenate([imag_part, real_part], axis=2)
    return jnp.concatenate([upper_rows, lower_rows], axis=1)

def small_solve(normal, right):
    factor = jnp.linalg.cholesky(normal)
    forward_vals = []
    for row_index in range(KRYLOV):
        partial_sum = right[row_index]
        for col_index in range(row_index):
            partial_sum = partial_sum - factor[row_index, col_index] * forward_vals[col_index]
        forward_vals.append(partial_sum / factor[row_index, row_index])
    backward_vals = [None] * KRYLOV
    for row_index in reversed(range(KRYLOV)):
        partial_sum = forward_vals[row_index]
        for col_index in range(row_index + 1, KRYLOV):
            partial_sum = partial_sum - factor[col_index, row_index] * backward_vals[col_index]
        backward_vals[row_index] = partial_sum / factor[row_index, row_index]
    return backward_vals

def reference(forward_coeff, incident, cost_grad, tmat_real, tmat_imag, translation_real, translation_imaginary, neighbours, particle_type):
    tmats = complex_blocks(tmat_real, tmat_imag)
    trans = complex_blocks(translation_real, translation_imaginary)
    tmat_adj = jnp.swapaxes(tmats, 1, 2)
    trans_adj = jnp.swapaxes(trans, 1, 2)
    kinds = jnp.arange(TYPES, dtype=jnp.int32)
    type_mask = (particle_type[None, :] == kinds[:, None]).astype(jnp.float32)
    target = jnp.where(neighbours >= 0, neighbours, NPART).astype(jnp.int32)

    def apply_adjoint(vector):
        scaled = jnp.zeros_like(vector)
        for kind_index in range(TYPES):
            scaled = scaled + type_mask[kind_index] * jnp.dot(tmat_adj[kind_index], vector, precision=HIGH)
        collected = jnp.zeros((COEFFICIENT_REAL, NPART + 1), jnp.float32)
        for neighbour_slot_index in range(NEIGHBOUR_SLOTS):
            collected = collected.at[:, target[neighbour_slot_index]].add(jnp.dot(trans_adj[neighbour_slot_index], scaled, precision=HIGH))
        return vector - collected[:, :NPART]
    padded_coeff = jnp.concatenate([forward_coeff, jnp.zeros((COEFFICIENT_REAL, 1), jnp.float32)], axis=1)
    exciting = incident
    for neighbour_slot_index in range(NEIGHBOUR_SLOTS):
        exciting = exciting + jnp.dot(trans[neighbour_slot_index], padded_coeff[:, target[neighbour_slot_index]], precision=HIGH)
    beta = jnp.sqrt(jnp.sum(cost_grad * cost_grad))
    basis = [cost_grad / beta]
    columns = []
    for column in range(KRYLOV):
        image = apply_adjoint(basis[column])
        projections = jnp.stack([jnp.sum(vec_item * image) for vec_item in basis])
        for row_index in range(column + 1):
            image = image - projections[row_index] * basis[row_index]
        height = jnp.sqrt(jnp.sum(image * image))
        columns.append(jnp.concatenate([projections, height[None], jnp.zeros((KRYLOV - column - 1,), jnp.float32)]))
        basis.append(image / height)
    hessen = jnp.stack(columns, axis=1)
    normal = jnp.dot(hessen.T, hessen, precision=HIGH)
    weights = small_solve(normal, beta * hessen[0])
    adjoint = weights[0] * basis[0]
    for column in range(1, KRYLOV):
        adjoint = adjoint + weights[column] * basis[column]
    sensitivity = jnp.stack([jnp.dot(adjoint * type_mask[kind_index], exciting.T, precision=HIGH) for kind_index in range(TYPES)])
    return (adjoint, sensitivity)
```

```python
import functools

import jax
import jax.numpy as jnp
from jax import lax
from jax.experimental import pallas as pl
from jax.experimental.pallas import tpu as pltpu
from jax.sharding import PartitionSpec as P

MESH = pl.DeviceIdType.MESH
COLS = 32
REACH = 2
F32 = jnp.float32
BF16 = jnp.bfloat16


def split(x):
    hi = x.astype(BF16)
    return hi, (x - hi.astype(F32)).astype(BF16)


def dot(a, b, rhs_dim=0):
    return lax.dot_general(a, b, (((1,), (rhs_dim,)), ((), ())), preferred_element_type=F32)


def dot3(a, b, rhs_dim=0):
    return dot(a[0], b[0], rhs_dim) + (dot(a[1], b[0], rhs_dim) + dot(a[0], b[1], rhs_dim))


def kernel(
    n_gx, n_gy, chunk,
    f_ref, inc_ref, g_ref, tr_ref, ti_ref, xr_ref, xi_ref, nbr_ref, kind_ref,
    adj_ref, sens_ref,
    t_hi, t_lo, w_hi, w_lo, one_ref, two_ref, y_hi, y_lo, fext, pack, coll, part, work,
    s_all, s_recv, s_mine, s_out, gram, gram_recv,
    f_send, f_recv, p_send, p_recv, gram_sem, rs_send, rs_recv, ag_sem,
):
    width, count = f_ref.shape
    half = width // 2
    kinds, slots = tr_ref.shape[0], xr_ref.shape[0]
    rows = count // COLS
    devices = n_gx * n_gy
    owners = kinds * width // chunk
    gx, gy = lax.axis_index("gx"), lax.axis_index("gy")
    me = gx * n_gy + gy

    def each_peer(body):
        def step(j, carry):
            peer = lax.rem(me + 1 + j, devices)
            body(j, peer, (peer // n_gy, lax.rem(peer, n_gy)))
            return carry
        lax.fori_loop(0, devices - 1, step, 0)

    barrier = pltpu.get_barrier_semaphore()
    each_peer(lambda j, peer, place: pl.semaphore_signal(
        barrier, inc=1, device_id=place, device_id_type=MESH))

    edge, side = REACH * COLS, REACH * rows
    above, below = (lax.rem(gx + n_gx - 1, n_gx), lax.rem(gx + 1, n_gx))
    left, right = (lax.rem(gy + n_gy - 1, n_gy), lax.rem(gy + 1, n_gy))
    blocks = (
        (0, edge, (above, gy), (below, gy)),
        (edge, edge, (below, gy), (above, gy)),
        (2 * edge, side, (gx, left), (gx, right)),
        (2 * edge + side, side, (gx, right), (gx, left)),
        (2 * edge + 2 * side, 8, (above, left), (below, right)),
        (2 * edge + 2 * side + 8, 8, (above, right), (below, left)),
        (2 * edge + 2 * side + 16, 8, (below, left), (above, right)),
        (2 * edge + 2 * side + 24, 8, (below, right), (above, left)),
    )
    small = 2 * edge
    last = COLS - REACH
    far = rows - REACH
    pieces = (
        (blocks[2][0], 0, rows, last),
        (blocks[3][0], 0, rows, 0),
        (blocks[4][0], far, REACH, last),
        (blocks[5][0], far, REACH, 0),
        (blocks[6][0], 0, REACH, last),
        (blocks[7][0], 0, REACH, 0),
    )

    fext[pl.ds(0, count), :] = f_ref[...].T
    pack[...] = jnp.zeros_like(pack)
    for start, row, number, column in pieces:
        for r in range(number):
            pack[pl.ds(start - small + REACH * r, REACH), :] = fext[
                pl.ds((row + r) * COLS + column, REACH), :]

    nbr = nbr_ref[...]
    tile, inner = nbr // count, nbr % count
    off_x, off_y = tile // n_gy - gx, tile % n_gy - gy
    row, col = inner // COLS, inner % COLS
    at_edge = jnp.where(off_x < 0, inner - (count - edge), inner + edge)
    at_side = 2 * edge + jnp.where(off_y < 0, 0, side) + row * REACH + jnp.where(off_y < 0, col - last, col)
    at_corner = (
        2 * edge + 2 * side + jnp.where(off_x < 0, 0, 16) + jnp.where(off_y < 0, 0, 8)
        + jnp.where(off_x < 0, row - far, row) * REACH + jnp.where(off_y < 0, col - last, col)
    )
    outside = jnp.where(off_y == 0, at_edge, jnp.where(off_x == 0, at_side, at_corner))
    target = jnp.where((off_x == 0) & (off_y == 0), inner, count + outside)
    target = jnp.where(nbr >= 0, target, -1)
    kind_row = kind_ref[...]
    pad = 16 - slots - 1
    meta = jnp.concatenate([target, kind_row] + ([jnp.zeros((pad, count), jnp.int32)] if pad else []), axis=0)
    meta_t = meta.astype(F32).T.astype(jnp.int32)
    extent = fext.shape[0]
    for s in range(slots):
        down = lax.broadcasted_iota(jnp.int32, (extent, count), 0)
        one_ref[:, pl.ds(s * count, count)] = jnp.where(down == target[s:s + 1, :], 1.0, 0.0).astype(BF16)
        across = lax.broadcasted_iota(jnp.int32, (count, extent), 1)
        two_ref[pl.ds(s * count, count), :] = jnp.where(across == meta_t[:, s:s + 1], 1.0, 0.0).astype(BF16)
    kind_col = meta_t[:, slots:slots + 1]

    def prepare(real_ref, imag_ref, hi_ref, lo_ref, number):
        for k in range(number):
            real, imag = real_ref[k], imag_ref[k]
            for start, block in (
                (0, jnp.concatenate([real, -imag], axis=1)),
                (half, jnp.concatenate([imag, real], axis=1)),
            ):
                hi, lo = split(block)
                hi_ref[k, pl.ds(start, half), :] = hi
                lo_ref[k, pl.ds(start, half), :] = lo

    prepare(tr_ref, ti_ref, t_hi, t_lo, kinds)
    prepare(xr_ref, xi_ref, w_hi, w_lo, slots)

    pl.semaphore_wait(barrier, devices - 1)

    f_copies = []
    for b, (start, size, _, place) in enumerate(blocks):
        if b == 0:
            src = fext.at[pl.ds(count - edge, edge)]
        elif b == 1:
            src = fext.at[pl.ds(0, edge)]
        else:
            src = pack.at[pl.ds(start - small, size)]
        copy = pltpu.make_async_remote_copy(
            src_ref=src, dst_ref=fext.at[pl.ds(count + start, size)],
            send_sem=f_send.at[b], recv_sem=f_recv.at[b], device_id=place, device_id_type=MESH)
        copy.start()
        f_copies.append(copy)

    def push(index, x):
        hi, lo = split(x)
        scaled = jnp.zeros((count, width), F32)
        for k in range(kinds):
            mask = jnp.where(kind_col == k, 1.0, 0.0).astype(BF16)
            scaled = scaled + dot3((hi * mask, lo * mask), (t_hi[k], t_lo[k]))
        pair = split(scaled)
        for s in range(slots):
            h, l = split(dot3(pair, (w_hi[s], w_lo[s])))
            y_hi[pl.ds(s * count, count), :] = h
            y_lo[pl.ds(s * count, count), :] = l
        coll[index] = dot(one_ref[...], y_hi[...]) + dot(one_ref[...], y_lo[...])
        copies = []
        for b, (start, size, place, _) in enumerate(blocks):
            copy = pltpu.make_async_remote_copy(
                src_ref=coll.at[index, pl.ds(count + start, size)], dst_ref=part.at[index, pl.ds(start, size)],
                send_sem=p_send.at[index, b], recv_sem=p_recv.at[index, b], device_id=place, device_id_type=MESH)
            copy.start()
            copies.append(copy)
        return copies

    def pull(index, copies):
        for copy in copies:
            copy.wait_recv()
        work[...] = coll[index, pl.ds(0, count), :]
        work[pl.ds(count - edge, edge), :] += part[index, pl.ds(0, edge), :]
        work[pl.ds(0, edge), :] += part[index, pl.ds(edge, edge), :]
        for start, row, number, column in pieces:
            for r in range(number):
                where = pl.ds((row + r) * COLS + column, REACH)
                work[where, :] += part[index, pl.ds(start + REACH * r, REACH), :]
        return work[...]

    def scatter_terms(index, field, exciting):
        hi, lo = split(field)
        for k in range(kinds):
            mask = jnp.where(kind_row == k, 1.0, 0.0).astype(BF16)
            s_all[index, pl.ds(k * width, width), :] = dot3((hi * mask, lo * mask), exciting)

        def send(j, peer, place):
            def go():
                pltpu.make_async_remote_copy(
                    src_ref=s_all.at[index, pl.ds(pl.multiple_of(peer * chunk, 8), chunk)],
                    dst_ref=s_recv.at[index, devices - 2 - j],
                    send_sem=rs_send.at[index], recv_sem=rs_recv.at[index],
                    device_id=place, device_id_type=MESH).start()
            if owners == devices:
                go()
            else:
                pl.when(peer < owners)(go)
        each_peer(send)

    def wait_bytes(sem, ref):
        pltpu.make_async_copy(ref, ref, sem).wait()

    g_t = g_ref[...].T
    first = push(0, g_t)

    for copy in f_copies:
        copy.wait_recv()
    ext = split(fext[...])
    exciting_t = inc_ref[...].T
    for s in range(slots):
        pick = two_ref[pl.ds(s * count, count), :]
        pair = (dot(pick, ext[0]).astype(BF16), dot(pick, ext[1]).astype(BF16))
        exciting_t = exciting_t + dot3(pair, (w_hi[s], w_lo[s]), 1)
    exciting = split(exciting_t)
    scatter_terms(0, g_ref[...], exciting)

    q0_t = pull(0, first)
    second = push(1, q0_t)
    q0 = q0_t.T
    scatter_terms(1, q0, exciting)
    q1_t = pull(1, second)

    for i, (a, b) in enumerate(
        ((g_t, g_t), (g_t, q0_t), (q0_t, q0_t), (g_t, q1_t), (q0_t, q1_t), (q1_t, q1_t))
    ):
        gram[i:i + 1, :] = jnp.sum(a * b, axis=0, keepdims=True)
    gram[6:8, :] = jnp.zeros((2, width), F32)
    each_peer(lambda j, peer, place: pltpu.make_async_remote_copy(
        src_ref=gram, dst_ref=gram_recv.at[devices - 2 - j],
        send_sem=gram_sem.at[0], recv_sem=gram_sem.at[1], device_id=place, device_id_type=MESH).start())
    wait_bytes(gram_sem.at[1], gram_recv)
    sums = jnp.sum(gram[...] + jnp.sum(gram_recv[...], axis=0), axis=1, keepdims=True)
    gg, gq, qq, gv, qv, vv = (sums[i:i + 1, :] for i in range(6))

    beta = jnp.sqrt(gg)
    c = gq / gg
    p2 = qq - c * gq
    p1 = jnp.sqrt(p2)
    gz = gv - c * gq
    pz = (qv - c * qq) - c * gz
    zz = vv - 2.0 * c * qv + c * c * qq
    h00, h10 = 1.0 - c, p1 / beta
    h01, h11 = gz / (beta * p1), 1.0 - pz / p2
    along = pz / p2
    h21 = jnp.sqrt(jnp.maximum(zz / p2 - h01 * h01 - along * along, 0.0))
    n00 = h00 * h00 + h10 * h10
    n01 = h00 * h01 + h10 * h11
    n11 = h01 * h01 + h11 * h11 + h21 * h21
    r0, r1 = beta * h00, beta * h01
    l00 = jnp.sqrt(n00)
    l10 = n01 / l00
    l11 = jnp.sqrt(n11 - l10 * l10)
    v0 = r0 / l00
    v1 = (r1 - l10 * v0) / l11
    w1 = v1 / l11
    w0 = (v0 - l10 * w1) / l00
    from_g, from_q = w0 / beta + w1 * c / p1, -w1 / p1
    adj_ref[...] = from_g * g_ref[...] + from_q * q0

    def reduce_mine():
        total = []
        for index in range(2):
            wait_bytes(rs_recv.at[index], s_recv.at[index])
            own = s_all[index, pl.ds(pl.multiple_of(me * chunk, 8), chunk), :]
            total.append(own + jnp.sum(s_recv[index], axis=0))
        mine = from_g * total[0] + from_q * total[1]
        s_mine[...] = mine
        each_peer(lambda j, peer, place: pltpu.make_async_remote_copy(
            src_ref=s_mine, dst_ref=s_out.at[pl.ds(pl.multiple_of(me * chunk, 8), chunk)],
            send_sem=ag_sem.at[0], recv_sem=ag_sem.at[1], device_id=place, device_id_type=MESH).start())
        s_out[pl.ds(pl.multiple_of(me * chunk, 8), chunk), :] = mine
        if owners > 1:
            wait_bytes(ag_sem.at[1], s_out.at[pl.ds(0, (owners - 1) * chunk)])
            for index in range(2):
                wait_bytes(rs_send.at[index], s_all.at[index, pl.ds(0, (owners - 1) * chunk)])
        wait_bytes(ag_sem.at[0], s_recv.at[0])

    if owners == devices:
        reduce_mine()
    else:
        pl.when(me < owners)(reduce_mine)

        @pl.when(me >= owners)
        def _():
            wait_bytes(ag_sem.at[1], s_out)
            for index in range(2):
                wait_bytes(rs_send.at[index], s_all.at[index])

    sens_ref[...] = s_out[...]
    for copy in f_copies + first + second:
        copy.wait_send()
    wait_bytes(gram_sem.at[0], gram_recv)


def body(n_gx, n_gy, forward_coeff, incident, cost_grad, tmat_real, tmat_imag, translation_real,
         translation_imaginary, neighbours, particle_type):
    width, count = forward_coeff.shape
    kinds, slots = tmat_real.shape[0], translation_real.shape[0]
    devices = n_gx * n_gy
    rows = count // COLS
    halo = 2 * REACH * COLS + 2 * REACH * rows + 32
    extent = count + halo
    total = kinds * width
    chunk = 8
    while total % chunk or total // chunk > devices:
        chunk += 8
    vmem = [pl.BlockSpec(memory_space=pltpu.VMEM)]
    adjoint, sensitivity = pl.pallas_call(
        functools.partial(kernel, n_gx, n_gy, chunk),
        out_shape=(
            jax.ShapeDtypeStruct((width, count), F32),
            jax.ShapeDtypeStruct((total, width), F32),
        ),
        in_specs=vmem * 9,
        out_specs=(vmem[0], vmem[0]),
        scratch_shapes=[
            pltpu.VMEM((kinds, width, width), BF16),
            pltpu.VMEM((kinds, width, width), BF16),
            pltpu.VMEM((slots, width, width), BF16),
            pltpu.VMEM((slots, width, width), BF16),
            pltpu.VMEM((extent, slots * count), BF16),
            pltpu.VMEM((slots * count, extent), BF16),
            pltpu.VMEM((slots * count, width), BF16),
            pltpu.VMEM((slots * count, width), BF16),
            pltpu.VMEM((extent, width), F32),
            pltpu.VMEM((2 * REACH * rows + 32, width), F32),
            pltpu.VMEM((2, extent, width), F32),
            pltpu.VMEM((2, halo, width), F32),
            pltpu.VMEM((count, width), F32),
            pltpu.VMEM((2, total, width), F32),
            pltpu.VMEM((2, devices - 1, chunk, width), F32),
            pltpu.VMEM((chunk, width), F32),
            pltpu.VMEM((total, width), F32),
            pltpu.VMEM((8, width), F32),
            pltpu.VMEM((devices - 1, 8, width), F32),
            pltpu.SemaphoreType.DMA((8,)),
            pltpu.SemaphoreType.DMA((8,)),
            pltpu.SemaphoreType.DMA((2, 8)),
            pltpu.SemaphoreType.DMA((2, 8)),
            pltpu.SemaphoreType.DMA((2,)),
            pltpu.SemaphoreType.DMA((2,)),
            pltpu.SemaphoreType.DMA((2,)),
            pltpu.SemaphoreType.DMA((2,)),
        ],
        compiler_params=pltpu.CompilerParams(
            collective_id=0, has_side_effects=True, vmem_limit_bytes=48 * 1024 * 1024),
    )(forward_coeff, incident, cost_grad, tmat_real, tmat_imag, translation_real,
      translation_imaginary, neighbours, particle_type.reshape(1, count))
    return adjoint, sensitivity.reshape(kinds, width, width)


def solution(mesh):
    spread = P(None, ("gx", "gy"))
    placed = (spread, spread, spread, P(), P(), P(), P(), spread, P(("gx", "gy")))
    return jax.shard_map(
        functools.partial(body, mesh.shape["gx"], mesh.shape["gy"]),
        mesh=mesh, in_specs=placed, out_specs=(spread, P()), check_vma=False)
```

```python
import functools

import jax
import jax.numpy as jnp
from jax import lax
from jax.experimental import pallas as pl
from jax.experimental.pallas import tpu as pltpu
from jax.sharding import PartitionSpec as P

MESH = pl.DeviceIdType.MESH
COLS = 32
REACH = 2
F32 = jnp.float32
BF16 = jnp.bfloat16


def split(x):
    hi = x.astype(BF16)
    return hi, (x - hi.astype(F32)).astype(BF16)


def dot(a, b, rhs_dim=0):
    return lax.dot_general(a, b, (((1,), (rhs_dim,)), ((), ())), preferred_element_type=F32)


def dot3(a, b, rhs_dim=0):
    return dot(a[0], b[0], rhs_dim) + (dot(a[1], b[0], rhs_dim) + dot(a[0], b[1], rhs_dim))


def kernel(
    n_gx, n_gy, chunk,
    f_ref, inc_ref, g_ref, tr_ref, ti_ref, xr_ref, xi_ref, nbr_ref, kind_ref,
    adj_ref, sens_ref,
    t_hi, t_lo, w_hi, w_lo, one_ref, two_ref, y_hi, y_lo, fext, pack, coll, part, work,
    s_all, s_twin, s_recv, s_mine, s_out, gram, gram_recv,
    f_send, f_recv, p_send, p_recv, gram_sem, twin_send, twin_recv, rs_send, rs_recv,
    ag_send, ag_recv, pass_sem,
):
    width, count = f_ref.shape
    half = width // 2
    kinds, slots = tr_ref.shape[0], xr_ref.shape[0]
    rows = count // COLS
    devices = n_gx * n_gy
    part_rows = kinds * width // 2
    owners = part_rows // chunk
    gx, gy = lax.axis_index("gx"), lax.axis_index("gy")
    me = gx * n_gy + gy

    def each_peer(body):
        def step(j, carry):
            peer = lax.rem(me + 1 + j, devices)
            body(j, peer, (peer // n_gy, lax.rem(peer, n_gy)))
            return carry
        lax.fori_loop(0, devices - 1, step, 0)

    core, team, mine = lax.rem(gy, 2), devices // 2, me // 2
    twin = (gx, gy + 1 - 2 * core)
    half_gy = n_gy // 2

    def each_mate(body):
        def step(j, carry):
            mate = lax.rem(mine + 1 + j, team)
            body(j, mate, (mate // half_gy, lax.rem(mate, half_gy) * 2 + core))
            return carry
        lax.fori_loop(0, team - 1, step, 0)

    def if_owner(number, act):
        if owners == team:
            act()
        else:
            pl.when(number < owners)(act)

    def chunk_of(number):
        return pl.ds(pl.multiple_of(number * chunk, 8), chunk)

    barrier = pltpu.get_barrier_semaphore()
    each_peer(lambda j, peer, place: pl.semaphore_signal(
        barrier, inc=1, device_id=place, device_id_type=MESH))

    edge, side = REACH * COLS, REACH * rows
    above, below = (lax.rem(gx + n_gx - 1, n_gx), lax.rem(gx + 1, n_gx))
    left, right = (lax.rem(gy + n_gy - 1, n_gy), lax.rem(gy + 1, n_gy))
    blocks = (
        (0, edge, (above, gy), (below, gy)),
        (edge, edge, (below, gy), (above, gy)),
        (2 * edge, side, (gx, left), (gx, right)),
        (2 * edge + side, side, (gx, right), (gx, left)),
        (2 * edge + 2 * side, 8, (above, left), (below, right)),
        (2 * edge + 2 * side + 8, 8, (above, right), (below, left)),
        (2 * edge + 2 * side + 16, 8, (below, left), (above, right)),
        (2 * edge + 2 * side + 24, 8, (below, right), (above, left)),
    )
    small = 2 * edge
    last = COLS - REACH
    far = rows - REACH
    pieces = (
        (blocks[2][0], 0, rows, last),
        (blocks[3][0], 0, rows, 0),
        (blocks[4][0], far, REACH, last),
        (blocks[5][0], far, REACH, 0),
        (blocks[6][0], 0, REACH, last),
        (blocks[7][0], 0, REACH, 0),
    )

    fext[pl.ds(0, count), :] = f_ref[...].T
    pack[...] = jnp.zeros_like(pack)
    for start, row, number, column in pieces:
        for r in range(number):
            pack[pl.ds(start - small + REACH * r, REACH), :] = fext[
                pl.ds((row + r) * COLS + column, REACH), :]

    nbr = nbr_ref[...]
    tile, inner = nbr // count, nbr % count
    off_x, off_y = tile // n_gy - gx, tile % n_gy - gy
    row, col = inner // COLS, inner % COLS
    at_edge = jnp.where(off_x < 0, inner - (count - edge), inner + edge)
    at_side = 2 * edge + jnp.where(off_y < 0, 0, side) + row * REACH + jnp.where(off_y < 0, col - last, col)
    at_corner = (
        2 * edge + 2 * side + jnp.where(off_x < 0, 0, 16) + jnp.where(off_y < 0, 0, 8)
        + jnp.where(off_x < 0, row - far, row) * REACH + jnp.where(off_y < 0, col - last, col)
    )
    outside = jnp.where(off_y == 0, at_edge, jnp.where(off_x == 0, at_side, at_corner))
    target = jnp.where((off_x == 0) & (off_y == 0), inner, count + outside)
    target = jnp.where(nbr >= 0, target, -1)
    kind_row = kind_ref[...]
    pad = 16 - slots - 1
    meta = jnp.concatenate([target, kind_row] + ([jnp.zeros((pad, count), jnp.int32)] if pad else []), axis=0)
    meta_t = meta.astype(F32).T.astype(jnp.int32)
    extent = fext.shape[0]
    for s in range(slots):
        down = lax.broadcasted_iota(jnp.int32, (extent, count), 0)
        one_ref[:, pl.ds(s * count, count)] = jnp.where(down == target[s:s + 1, :], 1.0, 0.0).astype(BF16)
        across = lax.broadcasted_iota(jnp.int32, (count, extent), 1)
        two_ref[pl.ds(s * count, count), :] = jnp.where(across == meta_t[:, s:s + 1], 1.0, 0.0).astype(BF16)
    kind_col = meta_t[:, slots:slots + 1]

    def prepare(real_ref, imag_ref, hi_ref, lo_ref, number):
        for k in range(number):
            real, imag = real_ref[k], imag_ref[k]
            for start, block in (
                (0, jnp.concatenate([real, -imag], axis=1)),
                (half, jnp.concatenate([imag, real], axis=1)),
            ):
                hi, lo = split(block)
                hi_ref[k, pl.ds(start, half), :] = hi
                lo_ref[k, pl.ds(start, half), :] = lo

    prepare(tr_ref, ti_ref, t_hi, t_lo, kinds)
    prepare(xr_ref, xi_ref, w_hi, w_lo, slots)

    pl.semaphore_wait(barrier, devices - 1)

    f_copies = []
    for b, (start, size, _, place) in enumerate(blocks):
        if b == 0:
            src = fext.at[pl.ds(count - edge, edge)]
        elif b == 1:
            src = fext.at[pl.ds(0, edge)]
        else:
            src = pack.at[pl.ds(start - small, size)]
        copy = pltpu.make_async_remote_copy(
            src_ref=src, dst_ref=fext.at[pl.ds(count + start, size)],
            send_sem=f_send.at[b], recv_sem=f_recv.at[b], device_id=place, device_id_type=MESH)
        copy.start()
        f_copies.append(copy)

    def push(index, x):
        hi, lo = split(x)
        scaled = jnp.zeros((count, width), F32)
        for k in range(kinds):
            mask = jnp.where(kind_col == k, 1.0, 0.0).astype(BF16)
            scaled = scaled + dot3((hi * mask, lo * mask), (t_hi[k], t_lo[k]))
        pair = split(scaled)
        for s in range(slots):
            h, l = split(dot3(pair, (w_hi[s], w_lo[s])))
            y_hi[pl.ds(s * count, count), :] = h
            y_lo[pl.ds(s * count, count), :] = l
        coll[index] = dot(one_ref[...], y_hi[...]) + dot(one_ref[...], y_lo[...])
        copies = []
        for b, (start, size, place, _) in enumerate(blocks):
            copy = pltpu.make_async_remote_copy(
                src_ref=coll.at[index, pl.ds(count + start, size)], dst_ref=part.at[index, pl.ds(start, size)],
                send_sem=p_send.at[index, b], recv_sem=p_recv.at[index, b], device_id=place, device_id_type=MESH)
            copy.start()
            copies.append(copy)
        return copies

    def pull(index, copies):
        for copy in copies:
            copy.wait_recv()
        work[...] = coll[index, pl.ds(0, count), :]
        work[pl.ds(count - edge, edge), :] += part[index, pl.ds(0, edge), :]
        work[pl.ds(0, edge), :] += part[index, pl.ds(edge, edge), :]
        for start, row, number, column in pieces:
            for r in range(number):
                where = pl.ds((row + r) * COLS + column, REACH)
                work[where, :] += part[index, pl.ds(start + REACH * r, REACH), :]
        return work[...]

    def gradient_terms(index, field, exciting):
        hi, lo = split(field)
        per = kinds // 2
        for where, base in ((0, 1 - core), (1, core)):
            for i in range(per):
                mask = jnp.where(kind_row == base * per + i, 1.0, 0.0).astype(BF16)
                s_all[index, where, pl.ds(i * width, width), :] = dot3((hi * mask, lo * mask), exciting)
            if where == 0:
                pltpu.make_async_remote_copy(
                    src_ref=s_all.at[index, 0], dst_ref=s_twin.at[index],
                    send_sem=twin_send.at[index], recv_sem=twin_recv.at[index],
                    device_id=twin, device_id_type=MESH).start()

    def send_terms(index):
        wait_bytes(twin_recv.at[index], s_twin.at[index])
        s_all[index, 1] += s_twin[index]

        def send(j, mate, place):
            if_owner(mate, lambda: pltpu.make_async_remote_copy(
                src_ref=s_all.at[index, 1, chunk_of(mate)], dst_ref=s_recv.at[index, team - 2 - j],
                send_sem=rs_send.at[index], recv_sem=rs_recv.at[index],
                device_id=place, device_id_type=MESH).start())
        each_mate(send)

    def wait_bytes(sem, ref):
        pltpu.make_async_copy(ref, ref, sem).wait()

    g_t = g_ref[...].T
    first = push(0, g_t)

    for copy in f_copies:
        copy.wait_recv()
    ext = split(fext[...])
    exciting_t = inc_ref[...].T
    for s in range(slots):
        pick = two_ref[pl.ds(s * count, count), :]
        pair = (dot(pick, ext[0]).astype(BF16), dot(pick, ext[1]).astype(BF16))
        exciting_t = exciting_t + dot3(pair, (w_hi[s], w_lo[s]), 1)
    exciting = split(exciting_t)
    gradient_terms(0, g_ref[...], exciting)

    q0_t = pull(0, first)
    send_terms(0)
    second = push(1, q0_t)
    q0 = q0_t.T
    gradient_terms(1, q0, exciting)
    q1_t = pull(1, second)

    lane = lax.broadcasted_iota(jnp.int32, (1, 128), 1)
    local = jnp.zeros((1, 128), F32)
    for i, (a, b) in enumerate(
        ((g_t, g_t), (g_t, q0_t), (q0_t, q0_t), (g_t, q1_t), (q0_t, q1_t), (q1_t, q1_t))
    ):
        product = jnp.sum(jnp.sum(a * b, axis=0, keepdims=True), axis=1, keepdims=True)
        local = jnp.where(lane == i, product, local)
    gram[...] = local
    each_peer(lambda j, peer, place: pltpu.make_async_remote_copy(
        src_ref=gram, dst_ref=gram_recv.at[devices - 2 - j],
        send_sem=gram_sem.at[0], recv_sem=gram_sem.at[1], device_id=place, device_id_type=MESH).start())
    send_terms(1)
    wait_bytes(gram_sem.at[1], gram_recv)
    sums = local + jnp.sum(gram_recv[...], axis=0)
    gg, gq, qq, gv, qv, vv = (sums[:, i:i + 1] for i in range(6))

    beta = jnp.sqrt(gg)
    c = gq / gg
    p2 = qq - c * gq
    p1 = jnp.sqrt(p2)
    gz = gv - c * gq
    pz = (qv - c * qq) - c * gz
    zz = vv - 2.0 * c * qv + c * c * qq
    h00, h10 = 1.0 - c, p1 / beta
    h01, h11 = gz / (beta * p1), 1.0 - pz / p2
    along = pz / p2
    h21 = jnp.sqrt(jnp.maximum(zz / p2 - h01 * h01 - along * along, 0.0))
    n00 = h00 * h00 + h10 * h10
    n01 = h00 * h01 + h10 * h11
    n11 = h01 * h01 + h11 * h11 + h21 * h21
    r0, r1 = beta * h00, beta * h01
    l00 = jnp.sqrt(n00)
    l10 = n01 / l00
    l11 = jnp.sqrt(n11 - l10 * l10)
    v0 = r0 / l00
    v1 = (r1 - l10 * v0) / l11
    w1 = v1 / l11
    w0 = (v0 - l10 * w1) / l00
    from_g, from_q = w0 / beta + w1 * c / p1, -w1 / p1
    adj_ref[...] = from_g * g_ref[...] + from_q * q0

    def hand_over(number):
        pltpu.make_async_remote_copy(
            src_ref=s_out.at[core, chunk_of(number)], dst_ref=s_out.at[core, chunk_of(number)],
            send_sem=pass_sem.at[0], recv_sem=pass_sem.at[1], device_id=twin, device_id_type=MESH).start()

    def reduce_mine():
        total = []
        for index in range(2):
            wait_bytes(rs_recv.at[index], s_recv.at[index])
            total.append(s_all[index, 1, chunk_of(mine), :] + jnp.sum(s_recv[index], axis=0))
        done = from_g * total[0] + from_q * total[1]
        s_mine[...] = done
        each_mate(lambda j, mate, place: pltpu.make_async_remote_copy(
            src_ref=s_mine, dst_ref=s_out.at[core, chunk_of(mine)],
            send_sem=ag_send.at[0], recv_sem=ag_recv.at[j], device_id=place, device_id_type=MESH).start())
        s_out[core, chunk_of(mine), :] = done
        hand_over(mine)

    if_owner(mine, reduce_mine)

    def relay(j, carry):
        source = lax.rem(mine - 1 - j + team, team)

        def act():
            wait_bytes(ag_recv.at[j], s_mine)
            hand_over(source)
        if_owner(source, act)
        return carry
    lax.fori_loop(0, team - 1, relay, 0)
    wait_bytes(pass_sem.at[1], s_out.at[0])

    for i in range(2):
        sens_ref[pl.ds(i * part_rows, part_rows), :] = s_out[i]
    for copy in f_copies + first + second:
        copy.wait_send()
    wait_bytes(gram_sem.at[0], gram_recv)
    wait_bytes(pass_sem.at[0], s_out.at[0])
    for index in range(2):
        wait_bytes(twin_send.at[index], s_all.at[index, 0])
    if owners > 1 or owners < team:
        def settle(number):
            if number:
                for index in range(2):
                    wait_bytes(rs_send.at[index], s_all.at[index, 0, pl.ds(0, number * chunk)])
        if owners == team:
            settle(owners - 1)
        else:
            pl.when(mine < owners)(lambda: settle(owners - 1))
            pl.when(mine >= owners)(lambda: settle(owners))
    if_owner(mine, lambda: wait_bytes(ag_send.at[0], s_recv.at[0]))


def body(n_gx, n_gy, forward_coeff, incident, cost_grad, tmat_real, tmat_imag, translation_real,
         translation_imaginary, neighbours, particle_type):
    width, count = forward_coeff.shape
    kinds, slots = tmat_real.shape[0], translation_real.shape[0]
    devices = n_gx * n_gy
    rows = count // COLS
    halo = 2 * REACH * COLS + 2 * REACH * rows + 32
    extent = count + halo
    total = kinds * width
    chunk = 8
    while (total // 2) % chunk or total // 2 // chunk > devices // 2:
        chunk += 8
    vmem = [pl.BlockSpec(memory_space=pltpu.VMEM)]
    adjoint, sensitivity = pl.pallas_call(
        functools.partial(kernel, n_gx, n_gy, chunk),
        out_shape=(
            jax.ShapeDtypeStruct((width, count), F32),
            jax.ShapeDtypeStruct((total, width), F32),
        ),
        in_specs=vmem * 9,
        out_specs=(vmem[0], vmem[0]),
        scratch_shapes=[
            pltpu.VMEM((kinds, width, width), BF16),
            pltpu.VMEM((kinds, width, width), BF16),
            pltpu.VMEM((slots, width, width), BF16),
            pltpu.VMEM((slots, width, width), BF16),
            pltpu.VMEM((extent, slots * count), BF16),
            pltpu.VMEM((slots * count, extent), BF16),
            pltpu.VMEM((slots * count, width), BF16),
            pltpu.VMEM((slots * count, width), BF16),
            pltpu.VMEM((extent, width), F32),
            pltpu.VMEM((2 * REACH * rows + 32, width), F32),
            pltpu.VMEM((2, extent, width), F32),
            pltpu.VMEM((2, halo, width), F32),
            pltpu.VMEM((count, width), F32),
            pltpu.VMEM((2, 2, total // 2, width), F32),
            pltpu.VMEM((2, total // 2, width), F32),
            pltpu.VMEM((2, devices // 2 - 1, chunk, width), F32),
            pltpu.VMEM((chunk, width), F32),
            pltpu.VMEM((2, total // 2, width), F32),
            pltpu.VMEM((1, 128), F32),
            pltpu.VMEM((devices - 1, 1, 128), F32),
            pltpu.SemaphoreType.DMA((8,)),
            pltpu.SemaphoreType.DMA((8,)),
            pltpu.SemaphoreType.DMA((2, 8)),
            pltpu.SemaphoreType.DMA((2, 8)),
            pltpu.SemaphoreType.DMA((2,)),
            pltpu.SemaphoreType.DMA((2,)),
            pltpu.SemaphoreType.DMA((2,)),
            pltpu.SemaphoreType.DMA((2,)),
            pltpu.SemaphoreType.DMA((2,)),
            pltpu.SemaphoreType.DMA((1,)),
            pltpu.SemaphoreType.DMA((devices // 2 - 1,)),
            pltpu.SemaphoreType.DMA((2,)),
        ],
        compiler_params=pltpu.CompilerParams(
            collective_id=0, has_side_effects=True, vmem_limit_bytes=48 * 1024 * 1024),
    )(forward_coeff, incident, cost_grad, tmat_real, tmat_imag, translation_real,
      translation_imaginary, neighbours, particle_type.reshape(1, count))
    return adjoint, sensitivity.reshape(kinds, width, width)


def solution(mesh):
    spread = P(None, ("gx", "gy"))
    placed = (spread, spread, spread, P(), P(), P(), P(), spread, P(("gx", "gy")))
    return jax.shard_map(
        functools.partial(body, mesh.shape["gx"], mesh.shape["gy"]),
        mesh=mesh, in_specs=placed, out_specs=(spread, P()), check_vma=False)
```

```python
import functools

import jax
import jax.numpy as jnp
from jax import lax
from jax.experimental import pallas as pl
from jax.experimental.pallas import tpu as pltpu
from jax.sharding import PartitionSpec as P

MESH = pl.DeviceIdType.MESH
COLS = 32
REACH = 2
F32 = jnp.float32
BF16 = jnp.bfloat16


def split(x):
    hi = x.astype(BF16)
    return hi, (x - hi.astype(F32)).astype(BF16)


def dot(a, b, rhs_dim=0):
    return lax.dot_general(a, b, (((1,), (rhs_dim,)), ((), ())), preferred_element_type=F32)


def dot3(a, b, rhs_dim=0):
    return dot(a[0], b[0], rhs_dim) + (dot(a[1], b[0], rhs_dim) + dot(a[0], b[1], rhs_dim))


def kernel(
    n_gx, n_gy, chunk,
    f_hbm, inc_hbm, g_hbm, tr_hbm, ti_hbm, xr_hbm, xi_hbm, nbr_hbm, kind_hbm,
    adj_ref, sens_ref,
    f_ref, inc_ref, g_ref, tr_ref, ti_ref, xr_ref, xi_ref, nbr_ref, kind_ref, load_sem,
    t_hi, t_lo, w_hi, w_lo, one_ref, two_ref, y_hi, y_lo, fext, pack, coll, part, work,
    s_all, s_twin, s_recv, s_mine, s_out, gram, gram_recv,
    f_send, f_recv, p_send, p_recv, gram_sem, twin_send, twin_recv, rs_send, rs_recv,
    ag_send, ag_recv, pass_sem,
):
    loads = [
        pltpu.make_async_copy(src, dst, load_sem.at[i])
        for i, (src, dst) in enumerate((
            (f_hbm, f_ref), (nbr_hbm, nbr_ref), (kind_hbm, kind_ref), (tr_hbm, tr_ref), (ti_hbm, ti_ref),
            (xr_hbm, xr_ref), (xi_hbm, xi_ref), (g_hbm, g_ref), (inc_hbm, inc_ref)))
    ]
    for load in loads:
        load.start()

    width, count = f_ref.shape
    half = width // 2
    kinds, slots = tr_ref.shape[0], xr_ref.shape[0]
    rows = count // COLS
    devices = n_gx * n_gy
    part_rows = kinds * width // 2
    owners = part_rows // chunk
    gx, gy = lax.axis_index("gx"), lax.axis_index("gy")
    me = gx * n_gy + gy

    def each_peer(body):
        def step(j, carry):
            peer = lax.rem(me + 1 + j, devices)
            body(j, peer, (peer // n_gy, lax.rem(peer, n_gy)))
            return carry
        lax.fori_loop(0, devices - 1, step, 0)

    core, team, mine = lax.rem(gy, 2), devices // 2, me // 2
    twin = (gx, gy + 1 - 2 * core)
    half_gy = n_gy // 2

    def each_mate(body):
        def step(j, carry):
            mate = lax.rem(mine + 1 + j, team)
            body(j, mate, (mate // half_gy, lax.rem(mate, half_gy) * 2 + core))
            return carry
        lax.fori_loop(0, team - 1, step, 0)

    def if_owner(number, act):
        if owners == team:
            act()
        else:
            pl.when(number < owners)(act)

    def chunk_of(number):
        return pl.ds(pl.multiple_of(number * chunk, 8), chunk)

    barrier = pltpu.get_barrier_semaphore()
    each_peer(lambda j, peer, place: pl.semaphore_signal(
        barrier, inc=1, device_id=place, device_id_type=MESH))

    edge, side = REACH * COLS, REACH * rows
    above, below = (lax.rem(gx + n_gx - 1, n_gx), lax.rem(gx + 1, n_gx))
    left, right = (lax.rem(gy + n_gy - 1, n_gy), lax.rem(gy + 1, n_gy))
    blocks = (
        (0, edge, (above, gy), (below, gy)),
        (edge, edge, (below, gy), (above, gy)),
        (2 * edge, side, (gx, left), (gx, right)),
        (2 * edge + side, side, (gx, right), (gx, left)),
        (2 * edge + 2 * side, 8, (above, left), (below, right)),
        (2 * edge + 2 * side + 8, 8, (above, right), (below, left)),
        (2 * edge + 2 * side + 16, 8, (below, left), (above, right)),
        (2 * edge + 2 * side + 24, 8, (below, right), (above, left)),
    )
    small = 2 * edge
    last = COLS - REACH
    far = rows - REACH
    pieces = (
        (blocks[2][0], 0, rows, last),
        (blocks[3][0], 0, rows, 0),
        (blocks[4][0], far, REACH, last),
        (blocks[5][0], far, REACH, 0),
        (blocks[6][0], 0, REACH, last),
        (blocks[7][0], 0, REACH, 0),
    )

    for load in loads[:3]:
        load.wait()
    fext[pl.ds(0, count), :] = f_ref[...].T
    pack[...] = jnp.zeros_like(pack)
    for start, row, number, column in pieces:
        for r in range(number):
            pack[pl.ds(start - small + REACH * r, REACH), :] = fext[
                pl.ds((row + r) * COLS + column, REACH), :]

    nbr = nbr_ref[...]
    tile, inner = nbr // count, nbr % count
    off_x, off_y = tile // n_gy - gx, tile % n_gy - gy
    row, col = inner // COLS, inner % COLS
    at_edge = jnp.where(off_x < 0, inner - (count - edge), inner + edge)
    at_side = 2 * edge + jnp.where(off_y < 0, 0, side) + row * REACH + jnp.where(off_y < 0, col - last, col)
    at_corner = (
        2 * edge + 2 * side + jnp.where(off_x < 0, 0, 16) + jnp.where(off_y < 0, 0, 8)
        + jnp.where(off_x < 0, row - far, row) * REACH + jnp.where(off_y < 0, col - last, col)
    )
    outside = jnp.where(off_y == 0, at_edge, jnp.where(off_x == 0, at_side, at_corner))
    target = jnp.where((off_x == 0) & (off_y == 0), inner, count + outside)
    target = jnp.where(nbr >= 0, target, -1)
    kind_row = kind_ref[...]
    pad = 16 - slots - 1
    meta = jnp.concatenate([target, kind_row] + ([jnp.zeros((pad, count), jnp.int32)] if pad else []), axis=0)
    meta_t = meta.astype(F32).T.astype(jnp.int32)
    extent = fext.shape[0]
    for s in range(slots):
        down = lax.broadcasted_iota(jnp.int32, (extent, count), 0)
        one_ref[:, pl.ds(s * count, count)] = jnp.where(down == target[s:s + 1, :], 1.0, 0.0).astype(BF16)
        across = lax.broadcasted_iota(jnp.int32, (count, extent), 1)
        two_ref[pl.ds(s * count, count), :] = jnp.where(across == meta_t[:, s:s + 1], 1.0, 0.0).astype(BF16)
    kind_col = meta_t[:, slots:slots + 1]

    def prepare(real_ref, imag_ref, hi_ref, lo_ref, number):
        for k in range(number):
            real, imag = real_ref[k], imag_ref[k]
            for start, block in (
                (0, jnp.concatenate([real, -imag], axis=1)),
                (half, jnp.concatenate([imag, real], axis=1)),
            ):
                hi, lo = split(block)
                hi_ref[k, pl.ds(start, half), :] = hi
                lo_ref[k, pl.ds(start, half), :] = lo

    for load in loads[3:]:
        load.wait()
    prepare(tr_ref, ti_ref, t_hi, t_lo, kinds)
    prepare(xr_ref, xi_ref, w_hi, w_lo, slots)

    pl.semaphore_wait(barrier, devices - 1)

    f_copies = []
    for b, (start, size, _, place) in enumerate(blocks):
        if b == 0:
            src = fext.at[pl.ds(count - edge, edge)]
        elif b == 1:
            src = fext.at[pl.ds(0, edge)]
        else:
            src = pack.at[pl.ds(start - small, size)]
        copy = pltpu.make_async_remote_copy(
            src_ref=src, dst_ref=fext.at[pl.ds(count + start, size)],
            send_sem=f_send.at[b], recv_sem=f_recv.at[b], device_id=place, device_id_type=MESH)
        copy.start()
        f_copies.append(copy)

    def push(index, x):
        hi, lo = split(x)
        scaled = jnp.zeros((count, width), F32)
        for k in range(kinds):
            mask = jnp.where(kind_col == k, 1.0, 0.0).astype(BF16)
            scaled = scaled + dot3((hi * mask, lo * mask), (t_hi[k], t_lo[k]))
        pair = split(scaled)
        for s in range(slots):
            h, l = split(dot3(pair, (w_hi[s], w_lo[s])))
            y_hi[pl.ds(s * count, count), :] = h
            y_lo[pl.ds(s * count, count), :] = l
        coll[index] = dot(one_ref[...], y_hi[...]) + dot(one_ref[...], y_lo[...])
        copies = []
        for b, (start, size, place, _) in enumerate(blocks):
            copy = pltpu.make_async_remote_copy(
                src_ref=coll.at[index, pl.ds(count + start, size)], dst_ref=part.at[index, pl.ds(start, size)],
                send_sem=p_send.at[index, b], recv_sem=p_recv.at[index, b], device_id=place, device_id_type=MESH)
            copy.start()
            copies.append(copy)
        return copies

    def pull(index, copies):
        for copy in copies:
            copy.wait_recv()
        work[...] = coll[index, pl.ds(0, count), :]
        work[pl.ds(count - edge, edge), :] += part[index, pl.ds(0, edge), :]
        work[pl.ds(0, edge), :] += part[index, pl.ds(edge, edge), :]
        for start, row, number, column in pieces:
            for r in range(number):
                where = pl.ds((row + r) * COLS + column, REACH)
                work[where, :] += part[index, pl.ds(start + REACH * r, REACH), :]
        return work[...]

    def gradient_terms(index, field, exciting):
        hi, lo = split(field)
        per = kinds // 2
        for where, base in ((0, 1 - core), (1, core)):
            for i in range(per):
                mask = jnp.where(kind_row == base * per + i, 1.0, 0.0).astype(BF16)
                s_all[index, where, pl.ds(i * width, width), :] = dot3((hi * mask, lo * mask), exciting)
            if where == 0:
                pltpu.make_async_remote_copy(
                    src_ref=s_all.at[index, 0], dst_ref=s_twin.at[index],
                    send_sem=twin_send.at[index], recv_sem=twin_recv.at[index],
                    device_id=twin, device_id_type=MESH).start()

    def send_terms(index):
        wait_bytes(twin_recv.at[index], s_twin.at[index])
        s_all[index, 1] += s_twin[index]

        def send(j, mate, place):
            if_owner(mate, lambda: pltpu.make_async_remote_copy(
                src_ref=s_all.at[index, 1, chunk_of(mate)], dst_ref=s_recv.at[index, team - 2 - j],
                send_sem=rs_send.at[index], recv_sem=rs_recv.at[index],
                device_id=place, device_id_type=MESH).start())
        each_mate(send)

    def wait_bytes(sem, ref):
        pltpu.make_async_copy(ref, ref, sem).wait()

    g_t = g_ref[...].T
    first = push(0, g_t)

    for copy in f_copies:
        copy.wait_recv()
    ext = split(fext[...])
    exciting_t = inc_ref[...].T
    for s in range(slots):
        pick = two_ref[pl.ds(s * count, count), :]
        pair = (dot(pick, ext[0]).astype(BF16), dot(pick, ext[1]).astype(BF16))
        exciting_t = exciting_t + dot3(pair, (w_hi[s], w_lo[s]), 1)
    exciting = split(exciting_t)
    gradient_terms(0, g_ref[...], exciting)

    q0_t = pull(0, first)
    send_terms(0)
    second = push(1, q0_t)
    q0 = q0_t.T
    gradient_terms(1, q0, exciting)
    q1_t = pull(1, second)

    lane = lax.broadcasted_iota(jnp.int32, (1, 128), 1)
    local = jnp.zeros((1, 128), F32)
    for i, (a, b) in enumerate(
        ((g_t, g_t), (g_t, q0_t), (q0_t, q0_t), (g_t, q1_t), (q0_t, q1_t), (q1_t, q1_t))
    ):
        product = jnp.sum(jnp.sum(a * b, axis=0, keepdims=True), axis=1, keepdims=True)
        local = jnp.where(lane == i, product, local)
    gram[...] = local
    each_peer(lambda j, peer, place: pltpu.make_async_remote_copy(
        src_ref=gram, dst_ref=gram_recv.at[devices - 2 - j],
        send_sem=gram_sem.at[0], recv_sem=gram_sem.at[1], device_id=place, device_id_type=MESH).start())
    send_terms(1)
    wait_bytes(gram_sem.at[1], gram_recv)
    sums = local + jnp.sum(gram_recv[...], axis=0)
    gg, gq, qq, gv, qv, vv = (sums[:, i:i + 1] for i in range(6))

    beta = jnp.sqrt(gg)
    c = gq / gg
    p2 = qq - c * gq
    p1 = jnp.sqrt(p2)
    gz = gv - c * gq
    pz = (qv - c * qq) - c * gz
    zz = vv - 2.0 * c * qv + c * c * qq
    h00, h10 = 1.0 - c, p1 / beta
    h01, h11 = gz / (beta * p1), 1.0 - pz / p2
    along = pz / p2
    h21 = jnp.sqrt(jnp.maximum(zz / p2 - h01 * h01 - along * along, 0.0))
    n00 = h00 * h00 + h10 * h10
    n01 = h00 * h01 + h10 * h11
    n11 = h01 * h01 + h11 * h11 + h21 * h21
    r0, r1 = beta * h00, beta * h01
    l00 = jnp.sqrt(n00)
    l10 = n01 / l00
    l11 = jnp.sqrt(n11 - l10 * l10)
    v0 = r0 / l00
    v1 = (r1 - l10 * v0) / l11
    w1 = v1 / l11
    w0 = (v0 - l10 * w1) / l00
    from_g, from_q = w0 / beta + w1 * c / p1, -w1 / p1
    adj_ref[...] = from_g * g_ref[...] + from_q * q0

    def hand_over(number):
        pltpu.make_async_remote_copy(
            src_ref=s_out.at[core, chunk_of(number)], dst_ref=s_out.at[core, chunk_of(number)],
            send_sem=pass_sem.at[0], recv_sem=pass_sem.at[1], device_id=twin, device_id_type=MESH).start()

    def reduce_mine():
        total = []
        for index in range(2):
            wait_bytes(rs_recv.at[index], s_recv.at[index])
            total.append(s_all[index, 1, chunk_of(mine), :] + jnp.sum(s_recv[index], axis=0))
        done = from_g * total[0] + from_q * total[1]
        s_mine[...] = done
        each_mate(lambda j, mate, place: pltpu.make_async_remote_copy(
            src_ref=s_mine, dst_ref=s_out.at[core, chunk_of(mine)],
            send_sem=ag_send.at[0], recv_sem=ag_recv.at[j], device_id=place, device_id_type=MESH).start())
        s_out[core, chunk_of(mine), :] = done
        hand_over(mine)

    if_owner(mine, reduce_mine)

    def relay(j, carry):
        source = lax.rem(mine - 1 - j + team, team)

        def act():
            wait_bytes(ag_recv.at[j], s_mine)
            hand_over(source)
        if_owner(source, act)
        return carry
    lax.fori_loop(0, team - 1, relay, 0)
    wait_bytes(pass_sem.at[1], s_out.at[0])

    for i in range(2):
        sens_ref[pl.ds(i * part_rows, part_rows), :] = s_out[i]
    for copy in f_copies + first + second:
        copy.wait_send()
    wait_bytes(gram_sem.at[0], gram_recv)
    wait_bytes(pass_sem.at[0], s_out.at[0])
    for index in range(2):
        wait_bytes(twin_send.at[index], s_all.at[index, 0])
    if owners > 1 or owners < team:
        def settle(number):
            if number:
                for index in range(2):
                    wait_bytes(rs_send.at[index], s_all.at[index, 0, pl.ds(0, number * chunk)])
        if owners == team:
            settle(owners - 1)
        else:
            pl.when(mine < owners)(lambda: settle(owners - 1))
            pl.when(mine >= owners)(lambda: settle(owners))
    if_owner(mine, lambda: wait_bytes(ag_send.at[0], s_recv.at[0]))


def body(n_gx, n_gy, forward_coeff, incident, cost_grad, tmat_real, tmat_imag, translation_real,
         translation_imaginary, neighbours, particle_type):
    width, count = forward_coeff.shape
    kinds, slots = tmat_real.shape[0], translation_real.shape[0]
    devices = n_gx * n_gy
    rows = count // COLS
    halo = 2 * REACH * COLS + 2 * REACH * rows + 32
    extent = count + halo
    total = kinds * width
    chunk = 8
    while (total // 2) % chunk or total // 2 // chunk > devices // 2:
        chunk += 8
    operands = (forward_coeff, incident, cost_grad, tmat_real, tmat_imag, translation_real,
                translation_imaginary, neighbours, particle_type.reshape(1, count))
    vmem = [pl.BlockSpec(memory_space=pltpu.VMEM)]
    adjoint, sensitivity = pl.pallas_call(
        functools.partial(kernel, n_gx, n_gy, chunk),
        out_shape=(
            jax.ShapeDtypeStruct((width, count), F32),
            jax.ShapeDtypeStruct((total, width), F32),
        ),
        in_specs=[pl.BlockSpec(memory_space=pltpu.HBM)] * 9,
        out_specs=(vmem[0], vmem[0]),
        scratch_shapes=[pltpu.VMEM(x.shape, x.dtype) for x in operands] + [
            pltpu.SemaphoreType.DMA((len(operands),)),
            pltpu.VMEM((kinds, width, width), BF16),
            pltpu.VMEM((kinds, width, width), BF16),
            pltpu.VMEM((slots, width, width), BF16),
            pltpu.VMEM((slots, width, width), BF16),
            pltpu.VMEM((extent, slots * count), BF16),
            pltpu.VMEM((slots * count, extent), BF16),
            pltpu.VMEM((slots * count, width), BF16),
            pltpu.VMEM((slots * count, width), BF16),
            pltpu.VMEM((extent, width), F32),
            pltpu.VMEM((2 * REACH * rows + 32, width), F32),
            pltpu.VMEM((2, extent, width), F32),
            pltpu.VMEM((2, halo, width), F32),
            pltpu.VMEM((count, width), F32),
            pltpu.VMEM((2, 2, total // 2, width), F32),
            pltpu.VMEM((2, total // 2, width), F32),
            pltpu.VMEM((2, devices // 2 - 1, chunk, width), F32),
            pltpu.VMEM((chunk, width), F32),
            pltpu.VMEM((2, total // 2, width), F32),
            pltpu.VMEM((1, 128), F32),
            pltpu.VMEM((devices - 1, 1, 128), F32),
            pltpu.SemaphoreType.DMA((8,)),
            pltpu.SemaphoreType.DMA((8,)),
            pltpu.SemaphoreType.DMA((2, 8)),
            pltpu.SemaphoreType.DMA((2, 8)),
            pltpu.SemaphoreType.DMA((2,)),
            pltpu.SemaphoreType.DMA((2,)),
            pltpu.SemaphoreType.DMA((2,)),
            pltpu.SemaphoreType.DMA((2,)),
            pltpu.SemaphoreType.DMA((2,)),
            pltpu.SemaphoreType.DMA((1,)),
            pltpu.SemaphoreType.DMA((devices // 2 - 1,)),
            pltpu.SemaphoreType.DMA((2,)),
        ],
        compiler_params=pltpu.CompilerParams(
            collective_id=0, has_side_effects=True, vmem_limit_bytes=67043328),
    )(*operands)
    return adjoint, sensitivity.reshape(kinds, width, width)


def solution(mesh):
    spread = P(None, ("gx", "gy"))
    placed = (spread, spread, spread, P(), P(), P(), P(), spread, P(("gx", "gy")))
    return jax.shard_map(
        functools.partial(body, mesh.shape["gx"], mesh.shape["gy"]),
        mesh=mesh, in_specs=placed, out_specs=(spread, P()), check_vma=False)
```
